32 devices in a mesh: req: 4 (over z), head: 8 (over y, x, core).
Axes of the slice: x: 2, y: 2, z: 4, core: 2. Of those that a mesh axis runs over, the one named last changes fastest.
Arguments:
- hidden_in: bfloat16 [64, 1024], P(('req', 'head')), may hold values from -6 to 6
- lengths: int32 [64], P('req'), may hold values from 2 to 1024, as said below
- request_order: int32 [64], replicated, may hold values from 0 to 63, each once
- key_cache: bfloat16 [2, 64, 16, 64, 1024], P(None, 'req', 'head')
- value_cache: bfloat16 [2, 64, 16, 64, 1024], P(None, 'req', 'head'), may hold values from -6 to 6
- w_qkv: bfloat16 [2, 16, 1024, 192], P(None, 'head'), may hold values from -0.1875 to 0.1875
- w_out: bfloat16 [2, 16, 64, 1024], P(None, 'head'), may hold values from -0.1875 to 0.1875
- w_up: bfloat16 [2, 1024, 4096], P(None, None, ('req', 'head')), may hold values from -0.1875 to 0.1875
- bias_up: bfloat16 [2, 4096], P(None, ('req', 'head')), may hold values from -3 to 3
- w_down: bfloat16 [2, 1024, 4096], P(None, None, ('req', 'head')), may hold values from -0.09375 to 0.09375
- norm_gain: float32 [2, 2, 1024], replicated, may hold values from 0.1 to 1.9
- norm_bias: float32 [2, 2, 1024], replicated, may hold values from -3 to 3
- embedding: bfloat16 [49152, 1024], P(('req', 'head')), may hold values from -0.59765625 to 0.59765625
Outputs:
- logits: float32 [64, 49152], P(None, ('req', 'head'))
The draws below stay inside these ranges and needn't reach their ends.
Inputs may be any that keep to these rules, and one draw needn't show every extreme that they name: `lengths`: the largest length is 1024. Slot s of the caches and of lengths belongs to request request_order[s]; each request once.
All inputs are finite; a program needn't handle non-finite values.
Results may differ from the reference program's by a relative error of at most 0.0095.
Values may be sent and summed in bfloat16 or wider, within the bound.
A program may use at most 64 MiB of HBM per device.

```python
import jax
import jax.numpy as jnp
from jax import lax

D = 1024
HEADS = 16
HEAD_DIM = 64
FF = 4096
VOCAB = 49152
LAYERS = 2
CACHE_MAX = 1024
REQUESTS = 64


def draw_lengths(key, part):
    first_key, second_key = jax.random.split(key)
    drawn = jax.random.randint(first_key, (REQUESTS,), 2, CACHE_MAX + 1)
    where_max = jax.random.randint(second_key, (), 0, REQUESTS)
    return drawn.at[where_max].set(CACHE_MAX).astype(jnp.int32)


def draw_key_cache(key, part):
    keys_all = jax.random.split(key, 1)
    shape_full = (LAYERS, REQUESTS, HEADS, HEAD_DIM, CACHE_MAX)
    base = jax.random.normal(keys_all[0], shape_full, jnp.float32)
    return base.astype(jnp.bfloat16)


def levels(key, extent, cuts, low, largest):
    def one(position, blocks):
        steps = jax.random.uniform(jax.random.fold_in(jax.random.fold_in(key, 6), position), (blocks,), jnp.float32, low / len(cuts), largest / len(cuts))
        return jnp.repeat(jnp.exp(steps), extent[position] // blocks).reshape((-1,) + (1,) * (len(extent) - position - 1))

    factor_of = one(*cuts[0])
    for cut in cuts[1:]:
        factor_of = factor_of * one(*cut)
    return factor_of


def gaussian(key, shape, width, bound, cuts=(), kind=jnp.bfloat16):
    entries = width * jax.random.normal(key, shape, jnp.float32)
    if cuts:
        entries = entries * levels(key, shape, cuts, -0.22, 0.18)
    return jnp.clip(entries, -bound, bound).astype(kind)


def setup_inputs(seed: int = 0) -> dict:
    splits = jax.random.split(jax.random.key(seed), 14)
    return {
        "hidden_in": gaussian(splits[0], (REQUESTS, D), 1.0, 6.0, ((0, 32),)),
        "lengths": draw_lengths(jax.random.fold_in(splits[13], 71), 0),
        "request_order": jax.random.permutation(splits[2], REQUESTS).astype(jnp.int32),
        "key_cache": draw_key_cache(jax.random.fold_in(splits[13], 71), 0),
        "value_cache": gaussian(splits[4], (LAYERS, REQUESTS, HEADS, HEAD_DIM, CACHE_MAX), 1.0, 6.0, ((1, 4), (2, 8))),
        "w_qkv": gaussian(splits[5], (LAYERS, HEADS, D, 3 * HEAD_DIM), D ** -0.5, 0.1875, ((1, 8),)),
        "w_out": gaussian(splits[6], (LAYERS, HEADS, HEAD_DIM, D), D ** -0.5, 0.1875, ((1, 8),)),
        "w_up": gaussian(splits[7], (LAYERS, D, FF), D ** -0.5, 0.1875, ((2, 32),)),
        "bias_up": gaussian(splits[8], (LAYERS, FF), 0.5, 3.0, ((1, 32),)),
        "w_down": gaussian(splits[9], (LAYERS, D, FF), FF ** -0.5, 0.09375, ((2, 32),)),
        "norm_gain": jnp.clip(1.0 + 0.18 * jax.random.normal(splits[10], (LAYERS, 2, D), jnp.float32), 0.1, 1.9),
        "norm_bias": gaussian(splits[11], (LAYERS, 2, D), 0.5, 3.0, (), jnp.float32),
        "embedding": gaussian(splits[12], (VOCAB, D), 0.1, 0.59765625, ((0, 32),)),
    }


def layer_norm(values, gain_vec, bias_vec):
    average = lax.optimization_barrier(jnp.mean(values, axis=-1, keepdims=True))
    centred = values - average
    variance = lax.optimization_barrier(jnp.mean(centred * centred, axis=-1, keepdims=True))
    return centred * lax.rsqrt(variance + 1e-05) * gain_vec + bias_vec

def one_head(query, own_key, own_value, keys, values, lengths, score_scale):
    positions = jnp.arange(CACHE_MAX, dtype=jnp.int32)
    scores = jnp.einsum('rd,rdl->rl', query, keys.astype(jnp.float32)) * score_scale
    scores = jnp.where(positions[None, :] < lengths[:, None], scores, -jnp.inf)
    own = lax.optimization_barrier(jnp.sum(query * own_key, axis=-1)) * score_scale
    row_max = jnp.maximum(lax.optimization_barrier(jnp.max(scores, axis=-1)), own)
    expo = jnp.exp(scores - row_max[:, None])
    own_exp = jnp.exp(own - row_max)
    denom = lax.optimization_barrier(jnp.sum(expo, axis=-1)) + own_exp
    expo_b = lax.optimization_barrier(expo.astype(jnp.bfloat16)).astype(jnp.float32)
    own_b = lax.optimization_barrier(own_exp.astype(jnp.bfloat16)).astype(jnp.float32)
    mixed = jnp.einsum('rl,rdl->rd', expo_b, values.astype(jnp.float32)) + own_b[:, None] * own_value
    return (mixed / denom[:, None]).astype(jnp.bfloat16)

def reference(hidden_in, lengths, request_order, key_cache, value_cache, w_qkv, w_out, w_up, bias_up, w_down, norm_gain, norm_bias, embedding):
    score_scale = HEAD_DIM ** (-0.5)
    state = hidden_in[request_order]
    for layer_idx in range(LAYERS):
        projected = jnp.einsum('rd,hde->rhe', state.astype(jnp.float32), w_qkv[layer_idx].astype(jnp.float32)).astype(jnp.bfloat16).astype(jnp.float32)
        outputs = []
        for head_idx in range(HEADS):
            outputs.append(one_head(projected[:, head_idx, :HEAD_DIM], projected[:, head_idx, HEAD_DIM:2 * HEAD_DIM], projected[:, head_idx, 2 * HEAD_DIM:], key_cache[layer_idx, :, head_idx], value_cache[layer_idx, :, head_idx], lengths, score_scale))
        head_out = jnp.stack(outputs, axis=1)
        attn_out = jnp.einsum('rhd,hde->re', head_out.astype(jnp.float32), w_out[layer_idx].astype(jnp.float32))
        normed = layer_norm(state.astype(jnp.float32) + attn_out, norm_gain[layer_idx, 0], norm_bias[layer_idx, 0]).astype(jnp.bfloat16)
        pre_act = jnp.dot(normed, w_up[layer_idx], preferred_element_type=jnp.float32) + bias_up[layer_idx].astype(jnp.float32)
        hidden = jax.nn.gelu(pre_act, approximate=False).astype(jnp.bfloat16)
        mlp_out = jnp.einsum('rf,df->rd', hidden.astype(jnp.float32), w_down[layer_idx].astype(jnp.float32))
        state = layer_norm(normed.astype(jnp.float32) + mlp_out, norm_gain[layer_idx, 1], norm_bias[layer_idx, 1]).astype(jnp.bfloat16)
    inverse = jnp.zeros_like(request_order).at[request_order].set(jnp.arange(REQUESTS, dtype=jnp.int32))
    return jnp.dot(state[inverse], embedding.T, preferred_element_type=jnp.float32)
```

```python
import functools

import jax
import jax.numpy as jnp
from jax import lax
from jax.experimental import pallas as pl
from jax.experimental.pallas import tpu as pltpu
from jax.sharding import PartitionSpec as P

LAYERS = 2
MESH = pl.DeviceIdType.MESH
F32 = jnp.float32
BF16 = jnp.bfloat16
NT = (((1,), (1,)), ((), ()))


def layer_norm(values, gain_vec, bias_vec):
    average = jnp.mean(values, axis=-1, keepdims=True)
    centred = values - average
    variance = jnp.mean(centred * centred, axis=-1, keepdims=True)
    return centred * lax.rsqrt(variance + 1e-05) * gain_vec + bias_vec


def kernel(
    n_req,
    n_head,
    hidden_ref,
    lengths_ref,
    order_ref,
    key_hbm,
    value_hbm,
    qkv_hbm,
    out_w_hbm,
    up_hbm,
    bias_up_ref,
    down_hbm,
    gain_ref,
    bias_ref,
    emb_hbm,
    logits_ref,
    key_v,
    value_v,
    qkv_v,
    out_w_v,
    up_v,
    down_v,
    emb_v,
    load_sem,
    emb_sem,
    stage,
    column,
    plane,
    spread,
    column_send,
    column_recv,
    plane_send,
    plane_recv,
    spread_send,
    spread_recv,
):
    me_r = lax.axis_index("req")
    me_h = lax.axis_index("head")
    rows, width = hidden_ref.shape
    group, heads, head_size, cached = key_v.shape[1:]
    slots = n_req * group

    barrier = pltpu.get_barrier_semaphore()
    for step in range(1, n_head):
        peer = lax.rem(me_h + step, n_head)
        pl.semaphore_signal(barrier, inc=1, device_id=(me_r, peer), device_id_type=MESH)
    for step in range(1, n_req):
        peer = lax.rem(me_r + step, n_req)
        pl.semaphore_signal(barrier, inc=1, device_id=(peer, me_h), device_id_type=MESH)

    pairs = ((qkv_hbm, qkv_v), (key_hbm, key_v), (value_hbm, value_v), (out_w_hbm, out_w_v), (up_hbm, up_v), (down_hbm, down_v))

    def load(layer, which):
        source, target = pairs[which]
        return pltpu.make_async_copy(source.at[layer], target.at[layer], load_sem.at[layer, which])

    for layer in range(LAYERS):
        for which in range(len(pairs)):
            load(layer, which).start()
    emb_load = pltpu.make_async_copy(emb_hbm, emb_v, emb_sem)
    emb_load.start()

    def sum_column(turn, partial):
        stage[turn] = partial.astype(BF16).reshape(n_req, group, width)
        copies = []
        for step in range(1, n_req):
            peer = lax.rem(me_r + step, n_req)
            copies.append(
                pltpu.make_async_remote_copy(
                    src_ref=stage.at[turn, peer],
                    dst_ref=column.at[turn, step - 1],
                    send_sem=column_send.at[turn, step - 1],
                    recv_sem=column_recv.at[turn, step - 1],
                    device_id=(peer, me_h),
                    device_id_type=MESH,
                )
            )
        for copy in copies:
            copy.start()
        total = stage[turn, me_r].astype(F32)
        for step, copy in enumerate(copies):
            copy.wait()
            total += column[turn, step].astype(F32)
        return total

    def sum_plane(turn, partial):
        plane[turn, me_h] = partial.astype(BF16)
        copies = []
        for step in range(1, n_head):
            peer = lax.rem(me_h + step, n_head)
            copies.append(
                pltpu.make_async_remote_copy(
                    src_ref=plane.at[turn, me_h],
                    dst_ref=plane.at[turn, me_h],
                    send_sem=plane_send.at[turn, step - 1],
                    recv_sem=plane_recv.at[turn, step - 1],
                    device_id=(me_r, peer),
                    device_id_type=MESH,
                )
            )
        for copy in copies:
            copy.start()
        for copy in copies:
            copy.wait()
        total = plane[turn, 0].astype(F32)
        for peer in range(1, n_head):
            total += plane[turn, peer].astype(F32)
        return total

    def gather_column(turn, mine):
        spread[turn, me_r] = mine
        copies = []
        for step in range(1, n_req):
            peer = lax.rem(me_r + step, n_req)
            copies.append(
                pltpu.make_async_remote_copy(
                    src_ref=spread.at[turn, me_r],
                    dst_ref=spread.at[turn, me_r],
                    send_sem=spread_send.at[turn, step - 1],
                    recv_sem=spread_recv.at[turn, step - 1],
                    device_id=(peer, me_h),
                    device_id_type=MESH,
                )
            )
        for copy in copies:
            copy.start()
        for copy in copies:
            copy.wait()
        return spread[turn].reshape(slots, width)

    order_row = order_ref[...]
    eye = lax.broadcasted_iota(jnp.int32, (slots, slots), 0) == lax.broadcasted_iota(
        jnp.int32, (slots, slots), 1
    )
    order_col = jnp.sum(
        jnp.where(eye, jnp.broadcast_to(order_row, (slots, slots)).astype(F32), 0.0), axis=1, keepdims=True
    )
    first_row = (me_r * n_head + me_h) * rows
    hidden = hidden_ref[...].astype(F32)
    placed = jnp.zeros((slots, width), F32)
    for row in range(rows):
        placed = jnp.where(
            order_col == (first_row + row).astype(F32),
            jnp.broadcast_to(hidden[row : row + 1, :], (slots, width)),
            placed,
        )

    pl.semaphore_wait(barrier, n_head + n_req - 2)
    state = sum_plane(0, sum_column(0, placed)).astype(BF16)

    row_ids = lax.broadcasted_iota(jnp.int32, (group, cached), 0)
    limit = jnp.zeros((group, cached), jnp.int32)
    for row in range(group):
        limit = jnp.where(row_ids == row, lengths_ref[row], limit)
    valid = lax.broadcasted_iota(jnp.int32, (group, cached), 1) < limit
    flat = group * head_size
    diagonal = lax.broadcasted_iota(jnp.int32, (group, flat), 0) == (
        lax.broadcasted_iota(jnp.int32, (group, flat), 1) // head_size
    )
    score_scale = head_size ** (-0.5)

    def layer_step(layer, state):
        load(layer, 0).wait()
        attn = jnp.zeros((group, width), F32)
        parts = []
        for head in range(heads):
            projected = jnp.dot(state, qkv_v[layer, head], preferred_element_type=F32).astype(BF16).astype(F32)
            parts.append(
                (
                    projected[:, :head_size],
                    projected[:, head_size : 2 * head_size],
                    projected[:, 2 * head_size :],
                )
            )
        load(layer, 1).wait()
        expos = []
        for head in range(heads):
            query, own_key, own_value = parts[head]
            tiled = jnp.where(diagonal, jnp.concatenate([query] * group, axis=1), 0.0).astype(BF16)
            keys = key_v[layer, :, head].reshape(flat, cached)
            scores = jnp.dot(tiled, keys, preferred_element_type=F32) * score_scale
            scores = jnp.where(valid, scores, -jnp.inf)
            own = jnp.sum(query * own_key, axis=-1, keepdims=True) * score_scale
            row_max = jnp.maximum(jnp.max(scores, axis=-1, keepdims=True), own)
            expo = jnp.exp(scores - row_max)
            own_exp = jnp.exp(own - row_max)
            denom = jnp.sum(expo, axis=-1, keepdims=True) + own_exp
            expos.append((expo.astype(BF16), own_exp.astype(BF16).astype(F32), denom))
        load(layer, 2).wait()
        load(layer, 3).wait()
        for head in range(heads):
            expo, own_exp, denom = expos[head]
            values = value_v[layer, :, head].reshape(flat, cached)
            every = lax.dot_general(expo, values, NT, preferred_element_type=F32)
            every = jnp.where(diagonal, every, 0.0)
            mixed = every[:, :head_size]
            for part in range(1, group):
                mixed += every[:, part * head_size : (part + 1) * head_size]
            mixed += own_exp * parts[head][2]
            head_out = (mixed / denom).astype(BF16)
            attn += jnp.dot(head_out, out_w_v[layer, head], preferred_element_type=F32)
        attn = sum_plane(1 + 2 * layer, attn)
        gains, biases = gain_ref[layer], bias_ref[layer]
        normed = layer_norm(state.astype(F32) + attn, gains[0:1], biases[0:1]).astype(BF16)
        everyone = gather_column(layer, normed)
        load(layer, 4).wait()
        bias_up = bias_up_ref[...].astype(F32)
        bias_row = bias_up[0:1]
        for other in range(1, LAYERS):
            bias_row = jnp.where(layer == other, bias_up[other : other + 1], bias_row)
        pre_act = jnp.dot(everyone, up_v[layer], preferred_element_type=F32) + bias_row
        hidden = (0.5 * pre_act * (1.0 + lax.erf(pre_act * 0.7071067811865476))).astype(BF16)
        load(layer, 5).wait()
        mlp = lax.dot_general(hidden, down_v[layer], NT, preferred_element_type=F32)
        mlp = sum_plane(2 + 2 * layer, sum_column(1 + layer, mlp))
        return layer_norm(normed.astype(F32) + mlp, gains[1:2], biases[1:2]).astype(BF16)

    state = lax.fori_loop(0, LAYERS, layer_step, state)
    everyone = gather_column(LAYERS, state)
    pick = (lax.broadcasted_iota(jnp.int32, (slots, slots), 0) == jnp.broadcast_to(order_row, (slots, slots))).astype(
        F32
    ).astype(BF16)
    ordered = jnp.dot(pick, everyone, preferred_element_type=F32).astype(BF16)
    emb_load.wait()
    logits_ref[...] = lax.dot_general(ordered, emb_v[...], NT, preferred_element_type=F32)


def body(n_req, n_head, *args):
    (hidden_in, lengths, request_order, key_cache, value_cache, w_qkv, w_out, w_up, bias_up, w_down) = args[:10]
    norm_gain, norm_bias, embedding = args[10:]
    group = lengths.shape[0]
    width = hidden_in.shape[1]
    slots = request_order.shape[0]
    vmem = pl.BlockSpec(memory_space=pltpu.VMEM)
    smem = pl.BlockSpec(memory_space=pltpu.SMEM)
    hbm = pl.BlockSpec(memory_space=pl.ANY)
    dma = pltpu.SemaphoreType.DMA
    held = [key_cache, value_cache, w_qkv, w_out, w_up, w_down, embedding]
    return pl.pallas_call(
        functools.partial(kernel, n_req, n_head),
        out_shape=jax.ShapeDtypeStruct((slots, embedding.shape[0]), F32),
        in_specs=[vmem, smem, vmem, hbm, hbm, hbm, hbm, hbm, vmem, hbm, vmem, vmem, hbm],
        out_specs=vmem,
        scratch_shapes=[pltpu.VMEM(array.shape, array.dtype) for array in held]
        + [
            dma((LAYERS, 6)),
            dma,
            pltpu.VMEM((1 + LAYERS, n_req, group, width), BF16),
            pltpu.VMEM((1 + LAYERS, n_req - 1, group, width), BF16),
            pltpu.VMEM((1 + 2 * LAYERS, n_head, group, width), BF16),
            pltpu.VMEM((1 + LAYERS, n_req, group, width), BF16),
            dma((1 + LAYERS, n_req - 1)),
            dma((1 + LAYERS, n_req - 1)),
            dma((1 + 2 * LAYERS, n_head - 1)),
            dma((1 + 2 * LAYERS, n_head - 1)),
            dma((1 + LAYERS, n_req - 1)),
            dma((1 + LAYERS, n_req - 1)),
        ],
        compiler_params=pltpu.CompilerParams(
            collective_id=0, has_side_effects=True, vmem_limit_bytes=56 * 1024 * 1024
        ),
    )(
        hidden_in,
        lengths,
        request_order.reshape(1, slots),
        key_cache,
        value_cache,
        w_qkv,
        w_out,
        w_up,
        bias_up,
        w_down,
        norm_gain,
        norm_bias,
        embedding,
    )


def solution(mesh):
    placed = (
        P(("req", "head"), None),
        P("req"),
        P(),
        P(None, "req", "head", None, None),
        P(None, "req", "head", None, None),
        P(None, "head", None, None),
        P(None, "head", None, None),
        P(None, None, ("req", "head")),
        P(None, ("req", "head")),
        P(None, None, ("req", "head")),
        P(),
        P(),
        P(("req", "head"), None),
    )
    return jax.shard_map(
        functools.partial(body, mesh.shape["req"], mesh.shape["head"]),
        mesh=mesh,
        in_specs=placed,
        out_specs=P(None, ("req", "head")),
        check_vma=False,
    )
```

```python
import functools

import jax
import jax.numpy as jnp
from jax import lax
from jax.experimental import pallas as pl
from jax.experimental.pallas import tpu as pltpu
from jax.sharding import PartitionSpec as P

LAYERS = 2
MESH = pl.DeviceIdType.MESH
F32 = jnp.float32
BF16 = jnp.bfloat16
NT = (((1,), (1,)), ((), ()))


def layer_norm(values, gain_vec, bias_vec):
    average = jnp.mean(values, axis=-1, keepdims=True)
    centred = values - average
    variance = jnp.mean(centred * centred, axis=-1, keepdims=True)
    return centred * lax.rsqrt(variance + 1e-05) * gain_vec + bias_vec


def peer_offsets(n_req, n_head):
    every = [(a, b) for a in range(n_req) for b in range(n_head) if a or b]
    return sorted(every, key=lambda o: (-(o[0] + bin(o[1] >> 1).count("1")), -o[1]))


def flip(index, mask):
    bit = 1
    while bit <= mask:
        if mask & bit:
            index = index + bit - 2 * bit * lax.rem(index // bit, 2)
        bit *= 2
    return index


def kernel(
    n_req,
    n_head,
    hidden_ref,
    lengths_ref,
    order_ref,
    key_hbm,
    value_hbm,
    qkv_hbm,
    out_w_hbm,
    up_hbm,
    bias_up_ref,
    down_hbm,
    gain_ref,
    bias_ref,
    emb_hbm,
    logits_ref,
    key_v,
    value_v,
    qkv_v,
    out_w_v,
    up_v,
    down_v,
    emb_v,
    load_sem,
    emb_sem,
    state_v,
    normed_v,
    first,
    attn_out,
    attn_in,
    spread,
    mlp_out,
    mlp_in,
    near,
    send_sem,
    recv_sem,
):
    me_r = lax.axis_index("req")
    me_h = lax.axis_index("head")
    me = me_r * n_head + me_h
    rows, width = hidden_ref.shape
    group, heads, head_size, cached = key_v.shape[1:]
    slots = n_req * group
    devices = n_req * n_head
    part = width // n_head
    offsets = peer_offsets(n_req, n_head)
    everywhere = [(flip(me_r, a), flip(me_h, b)) for a, b in offsets]
    plane = [(me_r, flip(me_h, b)) for a, b in offsets if not a]

    barrier = pltpu.get_barrier_semaphore()
    for peer in everywhere:
        pl.semaphore_signal(barrier, inc=1, device_id=peer, device_id_type=MESH)

    pairs = (
        (qkv_hbm, qkv_v),
        (key_hbm, key_v),
        (value_hbm, value_v),
        (out_w_hbm, out_w_v),
        (up_hbm, up_v),
        (down_hbm, down_v),
    )

    def load(layer, which):
        source, target = pairs[which]
        return pltpu.make_async_copy(source.at[layer], target.at[layer], load_sem.at[layer, which])

    for layer in range(LAYERS):
        for which in range(len(pairs)):
            load(layer, which).start()
    emb_load = pltpu.make_async_copy(emb_hbm, emb_v, emb_sem)
    emb_load.start()

    def send(turn, source, target, peers):
        for peer in peers:
            pltpu.make_async_remote_copy(
                src_ref=source(peer),
                dst_ref=target,
                send_sem=send_sem.at[turn],
                recv_sem=recv_sem.at[turn],
                device_id=peer,
                device_id_type=MESH,
            ).start()

    def wait(sem, turn, ref, count):
        block = ref.at[pl.ds(0, count)]
        pltpu.make_async_copy(block, block, sem.at[turn]).wait()

    chunks = width // 128
    tile = first.shape[1]
    hidden = hidden_ref[...].astype(F32)
    pieces = [hidden[:, c * 128 : (c + 1) * 128] for c in range(chunks)]
    if tile > chunks * rows:
        pieces.append(jnp.zeros((tile - chunks * rows, 128), F32))
    first[me] = jnp.concatenate(pieces, axis=0).astype(BF16)

    order_row = order_ref[...]
    ids_row = lax.broadcasted_iota(jnp.int32, (group, slots), 0) + me_r * group
    ids_col = lax.broadcasted_iota(jnp.int32, (group, slots), 1)
    order_here = jnp.sum(
        jnp.where(ids_row == ids_col, jnp.broadcast_to(order_row, (group, slots)).astype(F32), 0.0),
        axis=1,
        keepdims=True,
    ).astype(jnp.int32)
    wanted = (order_here // rows) * tile + lax.rem(order_here, rows)
    wide = lax.broadcasted_iota(jnp.int32, (group, devices * tile), 1)
    wanted = jnp.broadcast_to(wanted, (group, devices * tile))
    choose = jnp.concatenate(
        [(wide == wanted + c * rows).astype(F32) for c in range(chunks)], axis=0
    ).astype(BF16)

    row_ids = lax.broadcasted_iota(jnp.int32, (group, cached), 0)
    limit = jnp.zeros((group, cached), jnp.int32)
    for row in range(group):
        limit = jnp.where(row_ids == row, lengths_ref[row], limit)
    valid = lax.broadcasted_iota(jnp.int32, (group, cached), 1) < limit
    flat = group * head_size
    diagonal = lax.broadcasted_iota(jnp.int32, (group, flat), 0) == (
        lax.broadcasted_iota(jnp.int32, (group, flat), 1) // head_size
    )
    score_scale = head_size ** (-0.5)

    pl.semaphore_wait(barrier, devices - 1)
    send(0, lambda peer: first.at[me], first.at[me], everywhere)
    wait(recv_sem, 0, first, devices - 1)
    chosen = jnp.dot(choose, first[...].reshape(devices * tile, 128), preferred_element_type=F32)
    state = jnp.concatenate([chosen[c * group : (c + 1) * group] for c in range(chunks)], axis=1)
    for head in range(n_head):
        state_v[head] = state[:, head * part : (head + 1) * part].astype(BF16)

    def joined(ref, lead):
        return jnp.concatenate([ref[lead + (head,)] for head in range(n_head)], axis=1)

    def layer_step(layer, carry):
        attn_turn, spread_turn, mlp_turn, near_turn = 1 + 4 * layer, 2 + 4 * layer, 3 + 4 * layer, 4 + 4 * layer
        state = joined(state_v, ())
        load(layer, 0).wait()
        attn = jnp.zeros((group, width), F32)
        parts = []
        for head in range(heads):
            projected = (
                lax.dot_general(state, qkv_v[layer, head], NT, preferred_element_type=F32).astype(BF16).astype(F32)
            )
            parts.append(
                (
                    projected[:, :head_size],
                    projected[:, head_size : 2 * head_size],
                    projected[:, 2 * head_size :],
                )
            )
        load(layer, 1).wait()
        expos = []
        for head in range(heads):
            query, own_key, own_value = parts[head]
            tiled = jnp.where(diagonal, jnp.concatenate([query] * group, axis=1), 0.0).astype(BF16)
            keys = key_v[layer, :, head].reshape(flat, cached)
            scores = jnp.dot(tiled, keys, preferred_element_type=F32) * score_scale
            scores = jnp.where(valid, scores, -jnp.inf)
            own = jnp.sum(query * own_key, axis=-1, keepdims=True) * score_scale
            row_max = jnp.maximum(jnp.max(scores, axis=-1, keepdims=True), own)
            expo = jnp.exp(scores - row_max)
            own_exp = jnp.exp(own - row_max)
            denom = jnp.sum(expo, axis=-1, keepdims=True) + own_exp
            expos.append((expo.astype(BF16), own_exp.astype(BF16).astype(F32), denom))
        load(layer, 2).wait()
        load(layer, 3).wait()
        for head in range(heads):
            expo, own_exp, denom = expos[head]
            values = value_v[layer, :, head].reshape(flat, cached)
            every = lax.dot_general(expo, values, NT, preferred_element_type=F32)
            every = jnp.where(diagonal, every, 0.0)
            mixed = every[:, :head_size]
            for block in range(1, group):
                mixed += every[:, block * head_size : (block + 1) * head_size]
            mixed += own_exp * parts[head][2]
            head_out = (mixed / denom).astype(BF16)
            attn += jnp.dot(head_out, out_w_v[layer, head], preferred_element_type=F32)
        for head in range(n_head):
            attn_out[layer, head] = attn[:, head * part : (head + 1) * part].astype(BF16)
        send(attn_turn, lambda peer: attn_out.at[layer, peer[1]], attn_in.at[layer, me_h], plane)
        attn_in[layer, me_h] = attn_out[layer, me_h]
        wait(recv_sem, attn_turn, attn_in.at[layer], n_head - 1)
        total = attn_in[layer, 0].astype(F32)
        for head in range(1, n_head):
            total += attn_in[layer, head].astype(F32)
        spread[layer, me] = (total + state_v[me_h].astype(F32)).astype(BF16)
        send(spread_turn, lambda peer: spread.at[layer, me], spread.at[layer, me], everywhere)
        gains, biases = gain_ref[layer], bias_ref[layer]
        bias_up = bias_up_ref[...].astype(F32)
        bias_row = bias_up[0:1]
        for other in range(1, LAYERS):
            bias_row = jnp.where(layer == other, bias_up[other : other + 1], bias_row)
        load(layer, 4).wait()
        load(layer, 5).wait()
        wait(recv_sem, spread_turn, spread.at[layer], devices - 1)
        before = jnp.concatenate(
            [
                jnp.concatenate([spread[layer, req * n_head + head] for head in range(n_head)], axis=1)
                for req in range(n_req)
            ],
            axis=0,
        ).astype(F32)
        normed = layer_norm(before, gains[0:1], biases[0:1]).astype(BF16)
        for req in range(n_req):
            for head in range(n_head):
                normed_v[req * n_head + head] = normed[
                    req * group : (req + 1) * group, head * part : (head + 1) * part
                ]
        pre_act = jnp.dot(normed, up_v[layer], preferred_element_type=F32) + bias_row
        hidden = (0.5 * pre_act * (1.0 + lax.erf(pre_act * 0.7071067811865476))).astype(BF16)
        mlp = lax.dot_general(hidden, down_v[layer], NT, preferred_element_type=F32).astype(BF16)
        for req in range(n_req):
            for head in range(n_head):
                mlp_out[layer, req * n_head + head] = mlp[
                    req * group : (req + 1) * group, head * part : (head + 1) * part
                ]
        send(mlp_turn, lambda peer: mlp_out.at[layer, peer[0] * n_head + peer[1]], mlp_in.at[layer, me], everywhere)
        mlp_in[layer, me] = mlp_out[layer, me]
        wait(recv_sem, mlp_turn, mlp_in.at[layer], devices - 1)
        total = mlp_in[layer, 0].astype(F32)
        for device in range(1, devices):
            total += mlp_in[layer, device].astype(F32)
        after = (total + normed_v[me].astype(F32)).astype(BF16)

        @pl.when(layer < LAYERS - 1)
        def _():
            near[layer, me_h] = after
            send(near_turn, lambda peer: near.at[layer, me_h], near.at[layer, me_h], plane)
            wait(recv_sem, near_turn, near.at[layer], n_head - 1)
            fresh = joined(near, (layer,)).astype(F32)
            fresh = layer_norm(fresh, gains[1:2], biases[1:2]).astype(BF16)
            for head in range(n_head):
                state_v[head] = fresh[:, head * part : (head + 1) * part]

        @pl.when(layer == LAYERS - 1)
        def _():
            spread[LAYERS, me] = after

        return carry

    lax.fori_loop(0, LAYERS, layer_step, 0)
    last = 4 * LAYERS
    send(last, lambda peer: spread.at[LAYERS, me], spread.at[LAYERS, me], everywhere)
    pick = (
        (
            lax.broadcasted_iota(jnp.int32, (slots, slots), 0)
            == jnp.broadcast_to(order_row, (slots, slots))
        )
        .astype(F32)
        .astype(BF16)
    )
    emb_load.wait()
    wait(send_sem, 0, first, devices - 1)
    for layer in range(LAYERS):
        wait(send_sem, 1 + 4 * layer, attn_in.at[layer], n_head - 1)
        wait(send_sem, 2 + 4 * layer, spread.at[layer], devices - 1)
        wait(send_sem, 3 + 4 * layer, mlp_in.at[layer], devices - 1)
        if layer < LAYERS - 1:
            wait(send_sem, 4 + 4 * layer, near.at[layer], n_head - 1)
    wait(recv_sem, last, spread.at[LAYERS], devices - 1)
    before = jnp.concatenate(
        [
            jnp.concatenate([spread[LAYERS, req * n_head + head] for head in range(n_head)], axis=1)
            for req in range(n_req)
        ],
        axis=0,
    ).astype(F32)
    gains, biases = gain_ref[LAYERS - 1], bias_ref[LAYERS - 1]
    final = layer_norm(before, gains[1:2], biases[1:2]).astype(BF16)
    ordered = jnp.dot(pick, final, preferred_element_type=F32).astype(BF16)
    logits_ref[...] = lax.dot_general(ordered, emb_v[...], NT, preferred_element_type=F32)
    wait(send_sem, last, spread.at[LAYERS], devices - 1)


def body(n_req, n_head, *args):
    (hidden_in, lengths, request_order, key_cache, value_cache, w_qkv, w_out, w_up, bias_up, w_down) = args[:10]
    norm_gain, norm_bias, embedding = args[10:]
    group = lengths.shape[0]
    width = hidden_in.shape[1]
    w_qkv = jnp.swapaxes(w_qkv, 2, 3)
    slots = request_order.shape[0]
    devices = n_req * n_head
    part = width // n_head
    tile = max(16, hidden_in.shape[0] * width // 128)
    vmem = pl.BlockSpec(memory_space=pltpu.VMEM)
    smem = pl.BlockSpec(memory_space=pltpu.SMEM)
    hbm = pl.BlockSpec(memory_space=pl.ANY)
    dma = pltpu.SemaphoreType.DMA
    held = [key_cache, value_cache, w_qkv, w_out, w_up, w_down, embedding]
    return pl.pallas_call(
        functools.partial(kernel, n_req, n_head),
        out_shape=jax.ShapeDtypeStruct((slots, embedding.shape[0]), F32),
        in_specs=[vmem, smem, vmem, hbm, hbm, hbm, hbm, hbm, vmem, hbm, vmem, vmem, hbm],
        out_specs=vmem,
        scratch_shapes=[pltpu.VMEM(array.shape, array.dtype) for array in held]
        + [
            dma((LAYERS, 6)),
            dma,
            pltpu.VMEM((n_head, group, part), BF16),
            pltpu.VMEM((devices, group, part), BF16),
            pltpu.VMEM((devices, tile, 128), BF16),
            pltpu.VMEM((LAYERS, n_head, group, part), BF16),
            pltpu.VMEM((LAYERS, n_head, group, part), BF16),
            pltpu.VMEM((1 + LAYERS, devices, group, part), BF16),
            pltpu.VMEM((LAYERS, devices, group, part), BF16),
            pltpu.VMEM((LAYERS, devices, group, part), BF16),
            pltpu.VMEM((LAYERS, n_head, group, part), BF16),
            dma((1 + 4 * LAYERS,)),
            dma((1 + 4 * LAYERS,)),
        ],
        compiler_params=pltpu.CompilerParams(
            collective_id=0, has_side_effects=True, vmem_limit_bytes=56 * 1024 * 1024
        ),
    )(
        hidden_in,
        lengths,
        request_order.reshape(1, slots),
        key_cache,
        value_cache,
        w_qkv,
        w_out,
        w_up,
        bias_up,
        w_down,
        norm_gain,
        norm_bias,
        embedding,
    )


def solution(mesh):
    placed = (
        P(("req", "head"), None),
        P("req"),
        P(),
        P(None, "req", "head", None, None),
        P(None, "req", "head", None, None),
        P(None, "head", None, None),
        P(None, "head", None, None),
        P(None, None, ("req", "head")),
        P(None, ("req", "head")),
        P(None, None, ("req", "head")),
        P(),
        P(),
        P(("req", "head"), None),
    )
    return jax.shard_map(
        functools.partial(body, mesh.shape["req"], mesh.shape["head"]),
        mesh=mesh,
        in_specs=placed,
        out_specs=P(None, ("req", "head")),
        check_vma=False,
    )
```

```python
import functools

import jax
import jax.numpy as jnp
from jax import lax
from jax.experimental import pallas as pl
from jax.experimental.pallas import tpu as pltpu
from jax.sharding import PartitionSpec as P

LAYERS = 2
MESH = pl.DeviceIdType.MESH
F32 = jnp.float32
BF16 = jnp.bfloat16
NT = (((1,), (1,)), ((), ()))


def layer_norm(values, gain_vec, bias_vec):
    average = jnp.mean(values, axis=-1, keepdims=True)
    centred = values - average
    variance = jnp.mean(centred * centred, axis=-1, keepdims=True)
    return centred * lax.rsqrt(variance + 1e-05) * gain_vec + bias_vec


def peer_offsets(n_req, n_head):
    every = [(a, b) for a in range(n_req) for b in range(n_head) if a or b]
    return sorted(every, key=lambda o: (-(o[0] + bin(o[1] >> 1).count("1")), -o[1]))


def flip(index, mask):
    bit = 1
    while bit <= mask:
        if mask & bit:
            index = index + bit - 2 * bit * lax.rem(index // bit, 2)
        bit *= 2
    return index


def kernel(
    n_req,
    n_head,
    hidden_ref,
    lengths_ref,
    order_ref,
    key_hbm,
    value_hbm,
    qkv_hbm,
    out_w_hbm,
    up_hbm,
    bias_up_ref,
    down_hbm,
    gain_ref,
    bias_ref,
    emb_hbm,
    logits_ref,
    key_v,
    value_v,
    qkv_v,
    out_w_v,
    up_v,
    down_v,
    emb_v,
    load_sem,
    emb_sem,
    state_v,
    normed_v,
    first,
    attn_out,
    attn_in,
    spread,
    mlp_out,
    mlp_in,
    near,
    send_sem,
    recv_sem,
):
    me_r = lax.axis_index("req")
    me_h = lax.axis_index("head")
    me = me_r * n_head + me_h
    rows, width = hidden_ref.shape
    group, heads, head_size, cached = key_v.shape[1:]
    slots = n_req * group
    devices = n_req * n_head
    part = width // n_head
    offsets = peer_offsets(n_req, n_head)
    everywhere = [(flip(me_r, a), flip(me_h, b)) for a, b in offsets]
    plane = [(me_r, flip(me_h, b)) for a, b in offsets if not a]

    barrier = pltpu.get_barrier_semaphore()
    for peer in everywhere:
        pl.semaphore_signal(barrier, inc=1, device_id=peer, device_id_type=MESH)

    pairs = (
        (qkv_hbm, qkv_v),
        (key_hbm, key_v),
        (value_hbm, value_v),
        (out_w_hbm, out_w_v),
        (up_hbm, up_v),
        (down_hbm, down_v),
    )

    def load(layer, which):
        source, target = pairs[which]
        return pltpu.make_async_copy(source.at[layer], target.at[layer], load_sem.at[layer, which])

    for layer in range(LAYERS):
        for which in range(len(pairs)):
            load(layer, which).start()
    emb_load = pltpu.make_async_copy(emb_hbm, emb_v, emb_sem)
    emb_load.start()

    def send(turn, source, target, peers):
        for peer in peers:
            pltpu.make_async_remote_copy(
                src_ref=source(peer),
                dst_ref=target,
                send_sem=send_sem.at[turn],
                recv_sem=recv_sem.at[turn],
                device_id=peer,
                device_id_type=MESH,
            ).start()

    def wait(sem, turn, ref, count):
        block = ref.at[pl.ds(0, count)]
        pltpu.make_async_copy(block, block, sem.at[turn]).wait()

    chunks = width // 128
    tile = first.shape[1]
    hidden = hidden_ref[...].astype(F32)
    pieces = [hidden[:, c * 128 : (c + 1) * 128] for c in range(chunks)]
    if tile > chunks * rows:
        pieces.append(jnp.zeros((tile - chunks * rows, 128), F32))
    first[me] = jnp.concatenate(pieces, axis=0).astype(BF16)

    order_row = order_ref[...]
    ids_row = lax.broadcasted_iota(jnp.int32, (group, slots), 0) + me_r * group
    ids_col = lax.broadcasted_iota(jnp.int32, (group, slots), 1)
    order_here = jnp.sum(
        jnp.where(ids_row == ids_col, jnp.broadcast_to(order_row, (group, slots)).astype(F32), 0.0),
        axis=1,
        keepdims=True,
    ).astype(jnp.int32)
    wanted = (order_here // rows) * tile + lax.rem(order_here, rows)
    wide = lax.broadcasted_iota(jnp.int32, (group, devices * tile), 1)
    wanted = jnp.broadcast_to(wanted, (group, devices * tile))
    choose = jnp.concatenate(
        [(wide == wanted + c * rows).astype(F32) for c in range(chunks)], axis=0
    ).astype(BF16)

    square = lax.broadcasted_iota(jnp.int32, (group, group), 0) == lax.broadcasted_iota(
        jnp.int32, (group, group), 1
    )
    limit = jnp.sum(
        jnp.where(square, jnp.broadcast_to(lengths_ref[...], (group, group)).astype(F32), 0.0), axis=1, keepdims=True
    ).astype(jnp.int32)
    limit = jnp.broadcast_to(limit, (group, cached))
    valid = lax.broadcasted_iota(jnp.int32, (group, cached), 1) < limit
    flat = group * head_size
    diagonal = lax.broadcasted_iota(jnp.int32, (group, flat), 0) == (
        lax.broadcasted_iota(jnp.int32, (group, flat), 1) // head_size
    )
    score_scale = head_size ** (-0.5)

    pl.semaphore_wait(barrier, devices - 1)
    send(0, lambda peer: first.at[me], first.at[me], everywhere)
    wait(recv_sem, 0, first, devices - 1)
    chosen = jnp.dot(choose, first[...].reshape(devices * tile, 128), preferred_element_type=F32)
    state = jnp.concatenate([chosen[c * group : (c + 1) * group] for c in range(chunks)], axis=1)
    for head in range(n_head):
        state_v[head] = state[:, head * part : (head + 1) * part].astype(BF16)

    def joined(ref, lead):
        return jnp.concatenate([ref[lead + (head,)] for head in range(n_head)], axis=1)

    def layer_step(layer, carry):
        attn_turn, spread_turn, mlp_turn, near_turn = 1 + 4 * layer, 2 + 4 * layer, 3 + 4 * layer, 4 + 4 * layer
        state = joined(state_v, ())
        load(layer, 0).wait()
        attn = jnp.zeros((group, width), F32)
        parts = []
        for head in range(heads):
            projected = (
                lax.dot_general(state, qkv_v[layer, head], NT, preferred_element_type=F32).astype(BF16).astype(F32)
            )
            parts.append(
                (
                    projected[:, :head_size],
                    projected[:, head_size : 2 * head_size],
                    projected[:, 2 * head_size :],
                )
            )
        load(layer, 1).wait()
        expos = []
        for head in range(heads):
            query, own_key, own_value = parts[head]
            tiled = jnp.where(diagonal, jnp.concatenate([query] * group, axis=1), 0.0).astype(BF16)
            keys = key_v[layer, :, head].reshape(flat, cached)
            scores = jnp.dot(tiled, keys, preferred_element_type=F32) * score_scale
            scores = jnp.where(valid, scores, -jnp.inf)
            own = jnp.sum(query * own_key, axis=-1, keepdims=True) * score_scale
            row_max = jnp.maximum(jnp.max(scores, axis=-1, keepdims=True), own)
            expo = jnp.exp(scores - row_max)
            own_exp = jnp.exp(own - row_max)
            denom = jnp.sum(expo, axis=-1, keepdims=True) + own_exp
            expos.append((expo.astype(BF16), own_exp.astype(BF16).astype(F32), denom))
        load(layer, 2).wait()
        load(layer, 3).wait()
        for head in range(heads):
            expo, own_exp, denom = expos[head]
            values = value_v[layer, :, head].reshape(flat, cached)
            every = lax.dot_general(expo, values, NT, preferred_element_type=F32)
            every = jnp.where(diagonal, every, 0.0)
            mixed = every[:, :head_size]
            for block in range(1, group):
                mixed += every[:, block * head_size : (block + 1) * head_size]
            mixed += own_exp * parts[head][2]
            head_out = (mixed / denom).astype(BF16)
            attn += jnp.dot(head_out, out_w_v[layer, head], preferred_element_type=F32)
        for head in range(n_head):
            attn_out[layer, head] = attn[:, head * part : (head + 1) * part].astype(BF16)
        send(attn_turn, lambda peer: attn_out.at[layer, peer[1]], attn_in.at[layer, me_h], plane)
        attn_in[layer, me_h] = attn_out[layer, me_h]
        wait(recv_sem, attn_turn, attn_in.at[layer], n_head - 1)
        total = attn_in[layer, 0].astype(F32)
        for head in range(1, n_head):
            total += attn_in[layer, head].astype(F32)
        spread[layer, me] = (total + state_v[me_h].astype(F32)).astype(BF16)
        send(spread_turn, lambda peer: spread.at[layer, me], spread.at[layer, me], everywhere)
        gains, biases = gain_ref[layer], bias_ref[layer]
        bias_up = bias_up_ref[...].astype(F32)
        bias_row = bias_up[0:1]
        for other in range(1, LAYERS):
            bias_row = jnp.where(layer == other, bias_up[other : other + 1], bias_row)
        load(layer, 4).wait()
        load(layer, 5).wait()
        wait(recv_sem, spread_turn, spread.at[layer], devices - 1)
        before = jnp.concatenate(
            [
                jnp.concatenate([spread[layer, req * n_head + head] for head in range(n_head)], axis=1)
                for req in range(n_req)
            ],
            axis=0,
        ).astype(F32)
        normed = layer_norm(before, gains[0:1], biases[0:1]).astype(BF16)
        for req in range(n_req):
            for head in range(n_head):
                normed_v[req * n_head + head] = normed[
                    req * group : (req + 1) * group, head * part : (head + 1) * part
                ]
        pre_act = jnp.dot(normed, up_v[layer], preferred_element_type=F32) + bias_row
        hidden = (0.5 * pre_act * (1.0 + lax.erf(pre_act * 0.7071067811865476))).astype(BF16)
        mlp = lax.dot_general(hidden, down_v[layer], NT, preferred_element_type=F32).astype(BF16)
        for req in range(n_req):
            for head in range(n_head):
                mlp_out[layer, req * n_head + head] = mlp[
                    req * group : (req + 1) * group, head * part : (head + 1) * part
                ]
        send(mlp_turn, lambda peer: mlp_out.at[layer, peer[0] * n_head + peer[1]], mlp_in.at[layer, me], everywhere)
        mlp_in[layer, me] = mlp_out[layer, me]
        wait(recv_sem, mlp_turn, mlp_in.at[layer], devices - 1)
        total = mlp_in[layer, 0].astype(F32)
        for device in range(1, devices):
            total += mlp_in[layer, device].astype(F32)
        after = (total + normed_v[me].astype(F32)).astype(BF16)

        @pl.when(layer < LAYERS - 1)
        def _():
            near[layer, me_h] = after
            send(near_turn, lambda peer: near.at[layer, me_h], near.at[layer, me_h], plane)
            wait(recv_sem, near_turn, near.at[layer], n_head - 1)
            fresh = joined(near, (layer,)).astype(F32)
            fresh = layer_norm(fresh, gains[1:2], biases[1:2]).astype(BF16)
            for head in range(n_head):
                state_v[head] = fresh[:, head * part : (head + 1) * part]

        @pl.when(layer == LAYERS - 1)
        def _():
            spread[LAYERS, me] = after

        return carry

    lax.fori_loop(0, LAYERS, layer_step, 0)
    last = 4 * LAYERS
    send(last, lambda peer: spread.at[LAYERS, me], spread.at[LAYERS, me], everywhere)
    pick = (
        (
            lax.broadcasted_iota(jnp.int32, (slots, slots), 0)
            == jnp.broadcast_to(order_row, (slots, slots))
        )
        .astype(F32)
        .astype(BF16)
    )
    emb_load.wait()
    wait(send_sem, 0, first, devices - 1)
    for layer in range(LAYERS):
        wait(send_sem, 1 + 4 * layer, attn_in.at[layer], n_head - 1)
        wait(send_sem, 2 + 4 * layer, spread.at[layer], devices - 1)
        wait(send_sem, 3 + 4 * layer, mlp_in.at[layer], devices - 1)
        if layer < LAYERS - 1:
            wait(send_sem, 4 + 4 * layer, near.at[layer], n_head - 1)
    wait(recv_sem, last, spread.at[LAYERS], devices - 1)
    before = jnp.concatenate(
        [
            jnp.concatenate([spread[LAYERS, req * n_head + head] for head in range(n_head)], axis=1)
            for req in range(n_req)
        ],
        axis=0,
    ).astype(F32)
    gains, biases = gain_ref[LAYERS - 1], bias_ref[LAYERS - 1]
    final = layer_norm(before, gains[1:2], biases[1:2]).astype(BF16)
    ordered = jnp.dot(pick, final, preferred_element_type=F32).astype(BF16)
    logits_ref[...] = lax.dot_general(ordered, emb_v[...], NT, preferred_element_type=F32)
    wait(send_sem, last, spread.at[LAYERS], devices - 1)


def body(n_req, n_head, *args):
    (hidden_in, lengths, request_order, key_cache, value_cache, w_qkv, w_out, w_up, bias_up, w_down) = args[:10]
    norm_gain, norm_bias, embedding = args[10:]
    group = lengths.shape[0]
    width = hidden_in.shape[1]
    w_qkv = jnp.swapaxes(w_qkv, 2, 3)
    slots = request_order.shape[0]
    devices = n_req * n_head
    part = width // n_head
    tile = max(16, hidden_in.shape[0] * width // 128)
    vmem = pl.BlockSpec(memory_space=pltpu.VMEM)
    hbm = pl.BlockSpec(memory_space=pltpu.HBM)
    dma = pltpu.SemaphoreType.DMA
    pin = lambda array: pltpu.with_memory_space_constraint(array, pltpu.HBM)
    held = [key_cache, value_cache, w_qkv, w_out, w_up, w_down, embedding]
    return pl.pallas_call(
        functools.partial(kernel, n_req, n_head),
        out_shape=jax.ShapeDtypeStruct((slots, embedding.shape[0]), F32),
        in_specs=[vmem] * 3 + [hbm] * 5 + [vmem, hbm, vmem, vmem, hbm],
        out_specs=vmem,
        scratch_shapes=[pltpu.VMEM(array.shape, array.dtype) for array in held]
        + [
            dma((LAYERS, 6)),
            dma,
            pltpu.VMEM((n_head, group, part), BF16),
            pltpu.VMEM((devices, group, part), BF16),
            pltpu.VMEM((devices, tile, 128), BF16),
            pltpu.VMEM((LAYERS, n_head, group, part), BF16),
            pltpu.VMEM((LAYERS, n_head, group, part), BF16),
            pltpu.VMEM((1 + LAYERS, devices, group, part), BF16),
            pltpu.VMEM((LAYERS, devices, group, part), BF16),
            pltpu.VMEM((LAYERS, devices, group, part), BF16),
            pltpu.VMEM((LAYERS, n_head, group, part), BF16),
            dma((1 + 4 * LAYERS,)),
            dma((1 + 4 * LAYERS,)),
        ],
        compiler_params=pltpu.CompilerParams(
            collective_id=0, has_side_effects=True, vmem_limit_bytes=40 * 1024 * 1024
        ),
    )(
        pin(hidden_in),
        pin(lengths.reshape(1, group)),
        pin(request_order.reshape(1, slots)),
        pin(key_cache),
        pin(value_cache),
        pin(w_qkv),
        pin(w_out),
        pin(w_up),
        pin(bias_up),
        pin(w_down),
        pin(norm_gain),
        pin(norm_bias),
        pin(embedding),
    )


def solution(mesh):
    placed = (
        P(("req", "head"), None),
        P("req"),
        P(),
        P(None, "req", "head", None, None),
        P(None, "req", "head", None, None),
        P(None, "head", None, None),
        P(None, "head", None, None),
        P(None, None, ("req", "head")),
        P(None, ("req", "head")),
        P(None, None, ("req", "head")),
        P(),
        P(),
        P(("req", "head"), None),
    )
    return jax.shard_map(
        functools.partial(body, mesh.shape["req"], mesh.shape["head"]),
        mesh=mesh,
        in_specs=placed,
        out_specs=P(None, ("req", "head")),
        check_vma=False,
    )
```
